32 devices in a mesh: op: 4 (over y, x), str: 8 (over z, core).
Axes of the slice: x: 2, y: 2, z: 4, core: 2. Of those that a mesh axis runs over, the one named last changes fastest.
Arguments:
- coeffs: float32 [4096, 4096], P('str'), may hold values from -6 to 6
- previous: float32 [4096, 4096], P('str'), may hold values from -6 to 6
- block_values: bfloat16 [4, 32, 6, 128, 128], P('op'), may hold values from -0.21875 to 0.21875
- block_cols: int32 [4, 32, 6], P('op'), may hold values from 0 to 31, as said below
Outputs:
- advanced: float32 [4096, 4096], P('str')
The draws below stay inside these ranges and needn't reach their ends.
Inputs may be any that keep to these rules, and one draw needn't show every extreme that they name: For every term k and block row r, block_cols[k, r, 0] equals r and the 6 entries of block_cols[k, r] are distinct.
All inputs are finite; a program needn't handle non-finite values.
Results may differ from the reference program's by a relative error of at most 0.0003.
Values sent between devices are 32-bit elements; how exact they have to be, the bound alone decides.
A program may use at most 192 MiB of HBM per device.

```python
import math
import jax
import jax.numpy as jnp
from jax import lax

STRINGS = 4096
BLOCK = 128
BLOCKS = 32
ROW_BLOCKS = 6
TERMS = 4
STEPS = 2


def draw_block_cols(key, part):
    row_keys = jax.random.split(key, TERMS * BLOCKS)

    def one_row(row_key):
        return jax.random.permutation(row_key, BLOCKS - 1)[:ROW_BLOCKS - 1].astype(jnp.int32)
    others = jax.vmap(one_row)(row_keys).reshape(TERMS, BLOCKS, ROW_BLOCKS - 1)
    block_rows = jnp.arange(BLOCKS, dtype=jnp.int32)[None, :, None]
    others = (block_rows + 1 + others) % BLOCKS
    diagonal = jnp.broadcast_to(block_rows, (TERMS, BLOCKS, 1))
    return jnp.concatenate([diagonal, others], axis=2).astype(jnp.int32)


def shard_levels(rng, extent, shards, smallest, top_value):
    gain, own = 1.0, jax.random.fold_in(rng, 6)
    for dim, parts in shards:
        steps = jnp.exp(jax.random.uniform(jax.random.fold_in(own, dim), (parts,), jnp.float32, smallest / len(shards), top_value / len(shards)))
        gain = gain * jnp.repeat(steps, extent[dim] // parts).reshape([-1 if axis == dim else 1 for axis in range(len(extent))])
    return gain


def bell_draw(rng, extent, scale, most, pieces=(), held_as=jnp.bfloat16):
    gain = shard_levels(rng, extent, pieces, -0.22, 0.18) if pieces else 1.0
    drawn = jax.random.normal(rng, extent, jnp.float32) * scale * gain
    return jnp.minimum(jnp.maximum(drawn, -most), most).astype(held_as)


def setup_inputs(seed: int = 0) -> dict:
    arg_keys = jax.random.split(jax.random.key(seed), 5)
    return {
        "coeffs": bell_draw(arg_keys[0], (STRINGS, STRINGS), 1.0, 6.0, ((0, 8),), jnp.float32),
        "previous": bell_draw(arg_keys[1], (STRINGS, STRINGS), 1.0, 6.0, ((0, 8),), jnp.float32),
        "block_values": bell_draw(arg_keys[2], (TERMS, BLOCKS, ROW_BLOCKS, BLOCK, BLOCK), (ROW_BLOCKS * BLOCK) ** -0.5, 0.21875, ((0, 4),)),
        "block_cols": draw_block_cols(jax.random.fold_in(arg_keys[4], 71), 0),
    }


def apply_term(field, values, columns):
    factors = values.astype(jnp.float32)
    column_list = columns.reshape(-1)
    gathered = jnp.take(field.reshape(STRINGS, BLOCKS, BLOCK), column_list, axis=1)
    gathered = gathered.reshape(STRINGS, BLOCKS, ROW_BLOCKS, BLOCK)
    beta_side = jnp.einsum('arjc,rjoc->aro', gathered, factors, precision=lax.Precision.HIGHEST)
    beta_side = beta_side.reshape(STRINGS, STRINGS)
    grouped = jnp.take(beta_side.reshape(BLOCKS, BLOCK, STRINGS), column_list, axis=0)
    grouped = grouped.reshape(BLOCKS, ROW_BLOCKS, BLOCK, STRINGS)
    alpha_side = jnp.einsum('rjoc,rjcb->rob', factors, grouped, precision=lax.Precision.HIGHEST)
    return alpha_side.reshape(STRINGS, STRINGS)

def sigma_all(field, block_values, block_cols):

    def add_term(summed, term_pair):
        return (summed + apply_term(field, term_pair[0], term_pair[1]), None)
    summed, unused = lax.scan(add_term, jnp.zeros((STRINGS, STRINGS), jnp.float32), (block_values, block_cols))
    return summed

def reference(coeffs, previous, block_values, block_cols):
    step_scale = 2.0 / math.sqrt(TERMS)
    earlier, current = (previous, coeffs)
    for step_index in range(STEPS):
        updated = step_scale * sigma_all(current, block_values, block_cols) - earlier
        earlier, current = (current, updated)
    return current
```

```python
import functools
import math

import jax
import jax.numpy as jnp
from jax import lax
from jax.experimental import pallas as pl
from jax.experimental.pallas import tpu as pltpu
from jax.sharding import PartitionSpec as P

STEPS = 2
F32, BF16 = jnp.float32, jnp.bfloat16
VMEM_LIMIT = 60 * 1024 * 1024


def split(x):
    high = x.astype(BF16)
    return high, (x - high.astype(F32)).astype(BF16)


def call(body, grid, in_specs, out_specs, out_shape, scratch, flops, traffic):
    return pl.pallas_call(
        body,
        grid_spec=pltpu.PrefetchScalarGridSpec(
            num_scalar_prefetch=2,
            grid=grid,
            in_specs=in_specs,
            out_specs=out_specs,
            scratch_shapes=scratch,
        ),
        out_shape=out_shape,
        compiler_params=pltpu.CompilerParams(
            dimension_semantics=("arbitrary",), vmem_limit_bytes=VMEM_LIMIT
        ),
        cost_estimate=pl.CostEstimate(flops=flops, bytes_accessed=traffic, transcendentals=0),
    )


def whole(shape):
    return pl.BlockSpec(shape, lambda i, *_: (0,) * len(shape))


def operator_row(value_block, slots):
    return jnp.concatenate([value_block[j] for j in range(slots)], axis=1)


def beta_product(field, values, row, cols_ref, slots):
    left = jnp.concatenate([field[cols_ref[row * slots + j]] for j in range(slots)], axis=1)
    right = operator_row(values, slots)
    both = lax.dot_general(left, right, (((1,), (1,)), ((), ())), preferred_element_type=F32)
    m = both.shape[0] // 2
    return both[:m] + both[m:]


def alpha_product(field, values, row, cols_ref, slots):
    right = jnp.concatenate([field[cols_ref[row * slots + j]] for j in range(slots)], axis=0)
    both = jnp.dot(operator_row(values, slots), right, preferred_element_type=F32)
    n = both.shape[1] // 2
    return both[:, :n] + both[:, n:]


def beta_first(coeffs, previous, values, cols, place, chunk, shards, op_size):
    rows, width = coeffs.shape
    blocks, slots, block, _ = values.shape
    chunks = blocks // shards
    piece = rows // op_size

    def body(cols_ref, place_ref, v_ref, p_ref, a_ref, o_ref, field):
        i = pl.program_id(0)

        @pl.when(i == 0)
        def _():
            for b in range(blocks):
                high, low = split(v_ref[:, b * block : (b + 1) * block])
                field[b, :rows] = high
                field[b, rows:] = low

        o_ref[0, :rows] = beta_product(field, a_ref[0, 0], i * chunks + chunk, cols_ref, slots)
        o_ref[0, rows:] = p_ref[...]

    return call(
        body,
        (shards,),
        [
            whole((rows, width)),
            pl.BlockSpec((piece, block), lambda i, c, q: (q[0], i * chunks + chunk)),
            pl.BlockSpec((1, 1, slots, block, block), lambda i, *_: (i, chunk, 0, 0, 0)),
        ],
        pl.BlockSpec((1, rows + piece, block), lambda i, *_: (i, 0, 0)),
        jax.ShapeDtypeStruct((shards, rows + piece, block), F32),
        [pltpu.VMEM((blocks, 2 * rows, block), BF16)],
        4 * rows * slots * block * block * shards,
        4 * rows * width,
    )(cols, place, coeffs, previous, values.reshape(shards, chunks, slots, block, block))


def alpha_first(received, values, cols, place, scale, op_size):
    shards, deep, block = received.shape
    blocks, slots = values.shape[:2]
    chunks = blocks // shards
    rows = chunks * block
    piece = deep - rows
    group = 4

    def body(cols_ref, place_ref, w_ref, a_ref, o_ref, field):
        i = pl.program_id(0)

        @pl.when(i == 0)
        def _():
            for b in range(blocks):
                at = (b % chunks) * block
                high, low = split(w_ref[b // chunks, at : at + block])
                field[b, :, :block] = high
                field[b, :, block:] = low

        for g in range(group):
            row = i * group + g
            at = pl.multiple_of(lax.rem(row, chunks) * block, block)
            o_ref[lax.div(row, chunks), pl.ds(at, block)] = scale * alpha_product(
                field, a_ref[g], row, cols_ref, slots
            )

        @pl.when(i == blocks // group - 1)
        def _():
            at = pl.multiple_of(place_ref[0] * piece, piece)
            for s in range(shards):
                o_ref[s, pl.ds(at, piece)] = o_ref[s, pl.ds(at, piece)] - w_ref[s, rows:]

    return call(
        body,
        (blocks // group,),
        [
            whole((shards, deep, block)),
            pl.BlockSpec((group, slots, block, block), lambda i, *_: (i, 0, 0, 0)),
        ],
        whole((shards, rows, block)),
        jax.ShapeDtypeStruct((shards, rows, block), F32),
        [pltpu.VMEM((blocks, block, 2 * block), BF16)],
        4 * blocks * slots * block * block * block,
        8 * shards * rows * block,
    )(cols, place, received, values)


def alpha_second(currents, values, cols, place, chunk):
    shards, rows, block = currents[0].shape
    blocks, slots = values.shape[:2]
    chunks = blocks // shards
    wide = chunks * block

    def body(cols_ref, place_ref, *refs):
        v_refs, a_ref, o_ref, field = refs[:chunks], refs[chunks], refs[chunks + 1], refs[chunks + 2]
        i = pl.program_id(0)

        @pl.when(i == 0)
        def _():
            for c in range(chunks):
                for b in range(blocks):
                    at = (b % chunks) * block
                    high, low = split(v_refs[c][b // chunks, at : at + block])
                    field[b, :, c * block : (c + 1) * block] = high
                    field[b, :, wide + c * block : wide + (c + 1) * block] = low

        o_ref[0] = alpha_product(field, a_ref[0, 0], i * chunks + chunk, cols_ref, slots)

    return call(
        body,
        (shards,),
        [whole((shards, rows, block))] * chunks
        + [pl.BlockSpec((1, 1, slots, block, block), lambda i, *_: (i, chunk, 0, 0, 0))],
        pl.BlockSpec((1, block, wide), lambda i, *_: (i, 0, 0)),
        jax.ShapeDtypeStruct((shards, block, wide), F32),
        [pltpu.VMEM((blocks, block, 2 * wide), BF16)],
        4 * shards * slots * block * block * wide,
        4 * shards * rows * wide,
    )(cols, place, *currents, values.reshape(shards, chunks, slots, block, block))


def beta_second(received, coeffs, values, cols, place, scale, chunk, op_size):
    shards, block, wide = received.shape
    blocks, slots = values.shape[:2]
    chunks = blocks // shards
    width = shards * wide
    part = width // op_size
    group = 4

    def body(cols_ref, place_ref, u_ref, v_ref, a_ref, o_ref, field):
        i = pl.program_id(0)

        @pl.when(i == 0)
        def _():
            for b in range(blocks):
                at = (b % chunks) * block
                high, low = split(u_ref[b // chunks, :, at : at + block])
                field[b, :block] = high
                field[b, block:] = low

        for g in range(group):
            row = i * group + g
            o_ref[:, pl.ds(pl.multiple_of(row * block, block), block)] = scale * beta_product(
                field, a_ref[g], row, cols_ref, slots
            )

        @pl.when(i == blocks // group - 1)
        def _():
            at = pl.ds(pl.multiple_of(place_ref[0] * part, part), part)
            o_ref[:, at] = o_ref[:, at] - v_ref[...]

    return call(
        body,
        (blocks // group,),
        [
            whole((shards, block, wide)),
            pl.BlockSpec((block, part), lambda i, c, q: (chunk, q[0])),
            pl.BlockSpec((group, slots, block, block), lambda i, *_: (i, 0, 0, 0)),
        ],
        whole((block, width)),
        jax.ShapeDtypeStruct((block, width), F32),
        [pltpu.VMEM((blocks, 2 * block, block), BF16)],
        4 * blocks * slots * block * block * block,
        8 * width * block,
    )(cols, place, received, coeffs, values)


def per_device(coeffs, previous, block_values, block_cols):
    op_size, shards = lax.axis_size("op"), lax.axis_size("str")
    scale = 2.0 / math.sqrt(block_values.shape[0] * op_size)
    values = block_values[0]
    cols = block_cols[0].reshape(-1)
    place = lax.axis_index("op").astype(jnp.int32).reshape(1)
    chunks = values.shape[0] // shards

    swap = functools.partial(lax.all_to_all, axis_name="str", split_axis=0, concat_axis=0, tiled=True)
    def run(prepare, finish):
        moved, products, sums = [], [], []
        for chunk in range(chunks):
            sent = prepare(chunk)
            if chunk >= 1:
                sent, moved[chunk - 1] = lax.optimization_barrier((sent, moved[chunk - 1]))
            if chunk >= 2:
                product = finish(chunk - 2, moved[chunk - 2])
                sent, product = lax.optimization_barrier((sent, product))
                products.append(product)
            moved.append(swap(sent))
        for chunk in range(len(products), chunks):
            products.append(finish(chunk, moved[chunk]))
        for chunk in range(chunks):
            product = products[chunk]
            if chunk >= 1:
                product, sums[-1] = lax.optimization_barrier((product, sums[-1]))
            sums.append(lax.psum(product, "op"))
        return sums

    currents = run(
        lambda chunk: beta_first(coeffs, previous, values, cols, place, chunk, shards, op_size),
        lambda chunk, arrived: alpha_first(arrived, values, cols, place, scale, op_size),
    )
    outs = run(
        lambda chunk: alpha_second(currents, values, cols, place, chunk),
        lambda chunk, arrived: beta_second(
            arrived, coeffs, values, cols, place, scale, chunk, op_size
        ),
    )
    return jnp.concatenate(outs, axis=0)


def solution(mesh):
    placed = (P("str", None), P("str", None), P("op", None, None, None, None), P("op", None, None))
    return jax.shard_map(
        per_device, mesh=mesh, in_specs=placed, out_specs=P("str", None), check_vma=False
    )
```

```python
import functools
import math

import jax
import jax.numpy as jnp
from jax import lax
from jax.experimental import pallas as pl
from jax.experimental.pallas import tpu as pltpu
from jax.sharding import PartitionSpec as P

STEPS = 2
F32, BF16 = jnp.float32, jnp.bfloat16
VMEM_LIMIT = 60 * 1024 * 1024


def split(x):
    high = x.astype(BF16)
    return high, (x - high.astype(F32)).astype(BF16)


def call(body, grid, in_specs, out_specs, out_shape, scratch, flops, traffic):
    return pl.pallas_call(
        body,
        grid_spec=pltpu.PrefetchScalarGridSpec(
            num_scalar_prefetch=2,
            grid=grid,
            in_specs=in_specs,
            out_specs=out_specs,
            scratch_shapes=scratch,
        ),
        out_shape=out_shape,
        compiler_params=pltpu.CompilerParams(
            dimension_semantics=("arbitrary",), vmem_limit_bytes=VMEM_LIMIT
        ),
        cost_estimate=pl.CostEstimate(flops=flops, bytes_accessed=traffic, transcendentals=0),
    )


def whole(shape):
    return pl.BlockSpec(shape, lambda i, *_: (0,) * len(shape))


def operator_row(value_block, slots):
    return jnp.concatenate([value_block[j] for j in range(slots)], axis=1)


def beta_product(field, values, row, cols_ref, slots):
    left = jnp.concatenate([field[cols_ref[row * slots + j]] for j in range(slots)], axis=1)
    right = operator_row(values, slots)
    both = lax.dot_general(left, right, (((1,), (1,)), ((), ())), preferred_element_type=F32)
    m = both.shape[0] // 2
    return both[:m] + both[m:]


def alpha_product(field, values, row, cols_ref, slots):
    right = jnp.concatenate([field[cols_ref[row * slots + j]] for j in range(slots)], axis=0)
    both = jnp.dot(operator_row(values, slots), right, preferred_element_type=F32)
    n = both.shape[1] // 2
    return both[:, :n] + both[:, n:]


def beta_first(coeffs, previous, values, cols, place, chunk, shards, op_size):
    rows, width = coeffs.shape
    blocks, slots, block, _ = values.shape
    chunks = blocks // shards
    piece = rows // op_size

    def body(cols_ref, place_ref, v_ref, p_ref, a_ref, o_ref, field):
        i = pl.program_id(0)

        @pl.when(i == 0)
        def _():
            for b in range(blocks):
                high, low = split(v_ref[:, b * block : (b + 1) * block])
                field[b, :rows] = high
                field[b, rows:] = low

        o_ref[0, :rows] = beta_product(field, a_ref[0, 0], i * chunks + chunk, cols_ref, slots)
        o_ref[0, rows:] = p_ref[...]

    return call(
        body,
        (shards,),
        [
            whole((rows, width)),
            pl.BlockSpec((piece, block), lambda i, c, q: (q[0], i * chunks + chunk)),
            pl.BlockSpec((1, 1, slots, block, block), lambda i, *_: (i, chunk, 0, 0, 0)),
        ],
        pl.BlockSpec((1, rows + piece, block), lambda i, *_: (i, 0, 0)),
        jax.ShapeDtypeStruct((shards, rows + piece, block), F32),
        [pltpu.VMEM((blocks, 2 * rows, block), BF16)],
        4 * rows * slots * block * block * shards,
        4 * rows * width,
    )(cols, place, coeffs, previous, values.reshape(shards, chunks, slots, block, block))


def alpha_first(received, values, cols, place, scale, op_size):
    shards, deep, block = received.shape
    blocks, slots = values.shape[:2]
    chunks = blocks // shards
    rows = chunks * block
    piece = deep - rows
    near = shards // op_size
    group = 4

    def body(cols_ref, place_ref, w_ref, a_ref, o_ref, field):
        i = pl.program_id(0)

        @pl.when(i == 0)
        def _():
            for b in range(blocks):
                at = (b % chunks) * block
                high, low = split(w_ref[b // chunks, at : at + block])
                field[b, :, :block] = high
                field[b, :, block:] = low

        for g in range(group):
            row = i * group + g
            at = pl.multiple_of(lax.rem(row, chunks) * block, block)
            s = lax.div(row, chunks)
            slot = lax.bitwise_xor(lax.div(s, near), place_ref[0])
            o_ref[slot, lax.rem(s, near), pl.ds(at, block)] = scale * alpha_product(
                field, a_ref[g], row, cols_ref, slots
            )

        @pl.when(i == blocks // group - 1)
        def _():
            at = pl.multiple_of(place_ref[0] * piece, piece)
            for s in range(shards):
                slot = lax.bitwise_xor(place_ref[0], s // near)
                here = (slot, s % near, pl.ds(at, piece))
                o_ref[here] = o_ref[here] - w_ref[s, rows:]

    return call(
        body,
        (blocks // group,),
        [
            whole((shards, deep, block)),
            pl.BlockSpec((group, slots, block, block), lambda i, *_: (i, 0, 0, 0)),
        ],
        whole((op_size, near, rows, block)),
        jax.ShapeDtypeStruct((op_size, near, rows, block), F32),
        [pltpu.VMEM((blocks, block, 2 * block), BF16)],
        4 * blocks * slots * block * block * block,
        8 * shards * rows * block,
    )(cols, place, received, values)


def alpha_second(currents, values, cols, place, chunk):
    op_size = len(currents[0])
    near, rows, block = currents[0][0].shape
    shards = near * op_size
    pieces = [piece for current in currents for piece in current]
    blocks, slots = values.shape[:2]
    chunks = blocks // shards
    wide = chunks * block

    def body(cols_ref, place_ref, *refs):
        v_refs, (a_ref, o_ref, field) = refs[: len(pieces)], refs[len(pieces) :]
        i = pl.program_id(0)

        @pl.when(i == 0)
        def _():
            for n, v_ref in enumerate(v_refs):
                c = n // op_size
                first = lax.bitwise_xor(place_ref[0], n % op_size) * (near * chunks)
                for b in range(near * chunks):
                    at = (b % chunks) * block
                    high, low = split(v_ref[b // chunks, at : at + block])
                    field[first + b, :, c * block : (c + 1) * block] = high
                    field[first + b, :, wide + c * block : wide + (c + 1) * block] = low

        o_ref[0] = alpha_product(field, a_ref[0, 0], i * chunks + chunk, cols_ref, slots)

    return call(
        body,
        (shards,),
        [whole((near, rows, block))] * len(pieces)
        + [pl.BlockSpec((1, 1, slots, block, block), lambda i, *_: (i, chunk, 0, 0, 0))],
        pl.BlockSpec((1, block, wide), lambda i, *_: (i, 0, 0)),
        jax.ShapeDtypeStruct((shards, block, wide), F32),
        [pltpu.VMEM((blocks, block, 2 * wide), BF16)],
        4 * shards * slots * block * block * wide,
        4 * shards * rows * wide,
    )(cols, place, *pieces, values.reshape(shards, chunks, slots, block, block))


def beta_second(received, coeffs, values, cols, place, scale, chunk, op_size):
    shards, block, wide = received.shape
    blocks, slots = values.shape[:2]
    chunks = blocks // shards
    width = shards * wide
    part = width // op_size
    group = 4

    def body(cols_ref, place_ref, u_ref, v_ref, a_ref, o_ref, field):
        i = pl.program_id(0)

        @pl.when(i == 0)
        def _():
            for b in range(blocks):
                at = (b % chunks) * block
                high, low = split(u_ref[b // chunks, :, at : at + block])
                field[b, :block] = high
                field[b, block:] = low

        for g in range(group):
            row = i * group + g
            start = row * block
            slot = lax.bitwise_xor(lax.div(start, part), place_ref[0])
            at = pl.multiple_of(lax.rem(start, part), block)
            o_ref[slot, :, pl.ds(at, block)] = scale * beta_product(
                field, a_ref[g], row, cols_ref, slots
            )

        @pl.when(i == blocks // group - 1)
        def _():
            o_ref[0] = o_ref[0] - v_ref[...]

    return call(
        body,
        (blocks // group,),
        [
            whole((shards, block, wide)),
            pl.BlockSpec((block, part), lambda i, c, q: (chunk, q[0])),
            pl.BlockSpec((group, slots, block, block), lambda i, *_: (i, 0, 0, 0)),
        ],
        whole((op_size, block, part)),
        jax.ShapeDtypeStruct((op_size, block, part), F32),
        [pltpu.VMEM((blocks, 2 * block, block), BF16)],
        4 * blocks * slots * block * block * block,
        8 * width * block,
    )(cols, place, received, coeffs, values)


def per_device(coeffs, previous, block_values, block_cols):
    op_size, shards = lax.axis_size("op"), lax.axis_size("str")
    scale = 2.0 / math.sqrt(block_values.shape[0] * op_size)
    values = block_values[0]
    cols = block_cols[0].reshape(-1)
    place = lax.axis_index("op").astype(jnp.int32).reshape(1)
    chunks = values.shape[0] // shards

    swap = functools.partial(lax.all_to_all, axis_name="str", split_axis=0, concat_axis=0, tiled=True)
    def pass_on(value, offset):
        return lax.ppermute(value, "op", [(i, i ^ offset) for i in range(op_size)])

    def add_up(product):
        own = product[0]
        for piece in [pass_on(product[d], d) for d in range(1, op_size)]:
            own = own + piece
        return own

    def hand_out(own):
        return [own] + [pass_on(own, d) for d in range(1, op_size)]

    def run(prepare, finish):
        moved, owns, sums = [], [], []
        for chunk in range(chunks):
            at = place
            if chunk >= 2:
                product = finish(chunk - 2, moved[chunk - 2])
                at, product = lax.optimization_barrier((at, product))
                owns.append(add_up(product))
            sent = prepare(chunk, at)
            if chunk >= 1:
                sent, moved[chunk - 1] = lax.optimization_barrier((sent, moved[chunk - 1]))
            if chunk >= 2:
                sent, owns[-1] = lax.optimization_barrier((sent, owns[-1]))
            if chunk >= 3:
                sent, sums[-1] = lax.optimization_barrier((sent, sums[-1]))
            if chunk >= 2:
                sums.append(hand_out(owns[-1]))
            moved.append(swap(sent))
        for chunk in range(len(owns), chunks):
            arrived = moved[chunk]
            if chunk == chunks - 1 and chunk >= 2:
                arrived, owns[-1], sums[-1] = lax.optimization_barrier(
                    (arrived, owns[-1], sums[-1])
                )
            if len(sums) < len(owns):
                sums.append(hand_out(owns[-1]))
            owns.append(add_up(finish(chunk, arrived)))
        sums.append(hand_out(owns[-1]))
        return sums

    currents = run(
        lambda chunk, at: beta_first(coeffs, previous, values, cols, at, chunk, shards, op_size),
        lambda chunk, arrived: alpha_first(arrived, values, cols, place, scale, op_size),
    )
    outs = run(
        lambda chunk, at: alpha_second(currents, values, cols, at, chunk),
        lambda chunk, arrived: beta_second(
            arrived, coeffs, values, cols, place, scale, chunk, op_size
        ),
    )
    block, part = outs[0][0].shape
    advanced = jnp.zeros(coeffs.shape, F32)
    for chunk, pieces in enumerate(outs):
        for d, piece in enumerate(pieces):
            column = lax.bitwise_xor(place[0], d) * part
            advanced = lax.dynamic_update_slice(advanced, piece, (chunk * block, column))
    return advanced


def solution(mesh):
    placed = (P("str", None), P("str", None), P("op", None, None, None, None), P("op", None, None))
    return jax.shard_map(
        per_device, mesh=mesh, in_specs=placed, out_specs=P("str", None), check_vma=False
    )
```
